32 devices in a mesh: section: 2 (over core), ctx: 4 (over y, x), tp: 4 (over z).
Axes of the slice: x: 2, y: 2, z: 4, core: 2. Of those that a mesh axis runs over, the one named last changes fastest.
Arguments:
- boundary: bfloat16 [2, 2, 512, 2048], P('section', None, ('ctx', 'tp')), may hold values from -6 to 6
- pair_of_rank: int32 [4], replicated, may hold values from 0 to 3, each once
- norm_gains: bfloat16 [2, 2, 2048], P('section'), may hold values from 0.099609375 to 1.8984375
- w_query: bfloat16 [2, 2048, 2048], P('section', None, 'tp'), may hold values from -0.125 to 0.125
- w_keyval: bfloat16 [2, 2048, 4, 128], P('section', None, 'tp'), may hold values from -0.125 to 0.125
- w_out: bfloat16 [2, 2048, 2048], P('section', 'tp'), may hold values from -2 to 2
- w_in: bfloat16 [2, 2048, 2, 5632], P('section', None, None, 'tp'), may hold values from -0.125 to 0.125
- w_down: bfloat16 [2, 5632, 2048], P('section', 'tp'), may hold values from -0.078125 to 0.078125
Outputs:
- ends: float32 [2, 2, 512, 2048], P('section', None, ('ctx', 'tp'))
- grad_gains: float32 [2, 2, 2048], P('section', None, 'ctx')
- grad_query: float32 [2, 2048, 2048], P('section', 'ctx', 'tp')
- grad_keyval: float32 [2, 2048, 4, 128], P('section', 'ctx', 'tp')
- grad_out: float32 [2, 2048, 2048], P('section', 'tp', 'ctx')
- grad_in: float32 [2, 2048, 2, 5632], P('section', 'ctx', None, 'tp')
- grad_down: float32 [2, 5632, 2048], P('section', 'tp', 'ctx')
The draws below stay inside these ranges and needn't reach their ends.
Inputs may be any that keep to these rules, and one draw needn't show every extreme that they name: pair_of_rank[r] = p means context rank r holds sequence blocks p and 7 - p of 64 tokens, the lower first; every pair is held once.
All inputs are finite; a program needn't handle non-finite values.
Results may differ from the reference program's by a relative error of at most 0.035.
Values may be sent and summed in bfloat16 or wider, within the bound.
No kernel may reach another device: no remote copies, remote signals or barrier semaphores. Data moves between devices by JAX's collectives and lax.ppermute only.
A program may use at most 256 MiB of HBM per device.

```python
import jax
import jax.numpy as jnp
from jax import lax

D = 2048
HQ = 32
KVH = 4
HD = 64
FF = 5632
BLK = 64
MICRO = 2
SEQ = 512
N_SECTION = 2
N_CTX = 4


def levels(rng, shape, cuts, least, top_value):
    def one(dim, parts):
        heights = jax.random.uniform(jax.random.fold_in(jax.random.fold_in(rng, 6), dim), (parts,), jnp.float32, least / len(cuts), top_value / len(cuts))
        return jnp.repeat(jnp.exp(heights), shape[dim] // parts).reshape((-1,) + (1,) * (len(shape) - dim - 1))

    level = one(*cuts[0])
    for cut in cuts[1:]:
        level = level * one(*cut)
    return level


def normal_values(own_key, dims, deviation, reach, shards=(), kind=jnp.bfloat16):
    entries = deviation * jax.random.normal(own_key, dims, jnp.float32)
    if shards:
        entries = entries * levels(own_key, dims, shards, -0.22, 0.18)
    return jnp.clip(entries, -reach, reach).astype(kind)


def setup_inputs(seed: int = 0) -> dict:
    splits = jax.random.split(jax.random.key(seed), 9)
    boundary = normal_values(splits[0], (N_SECTION, MICRO, SEQ, D), 1.0, 6.0, ((0, 2), (2, 16)))
    pair_of_rank = jax.random.permutation(splits[1], N_CTX).astype(jnp.int32)
    norm_gains = jnp.clip(1.0 + 0.18 * jax.random.normal(splits[2], (N_SECTION, 2, D), jnp.float32), 0.099609375, 1.8984375).astype(jnp.bfloat16)
    w_query = normal_values(splits[3], (N_SECTION, D, HQ * HD), D ** -0.5, 0.125, ((0, 2), (2, 4)))
    w_keyval = normal_values(splits[4], (N_SECTION, D, KVH, 2 * HD), D ** -0.5, 0.125, ((0, 2), (2, 4)))
    w_out = normal_values(splits[5], (N_SECTION, HQ * HD, D), (max(1, HQ * HD // 256)) ** -0.5, 2.0, ((0, 2), (1, 4)))
    w_in = normal_values(splits[6], (N_SECTION, D, 2, FF), D ** -0.5, 0.125, ((0, 2), (3, 4)))
    w_down = normal_values(splits[7], (N_SECTION, FF, D), FF ** -0.5, 0.078125, ((0, 2), (1, 4)))
    return dict(boundary=boundary, pair_of_rank=pair_of_rank, norm_gains=norm_gains, w_query=w_query, w_keyval=w_keyval, w_out=w_out, w_in=w_in, w_down=w_down)


EPSILON = 1e-05
ROPE_BASE = 10000.0
MASKED = -1e+30
HIGHEST = lax.Precision.HIGHEST

@jax.custom_vjp
def low(v):
    return lax.optimization_barrier(v.astype(jnp.bfloat16)).astype(jnp.float32)

@jax.custom_vjp
def low_back(v):
    return v

def low_keep(v):
    return (low(v), None)

def low_pass(kept, grad):
    return (grad,)

def back_keep(v):
    return (v, None)

def back_low(kept, grad):
    return (low(grad),)
low.defvjp(low_keep, low_pass)
low_back.defvjp(back_keep, back_low)

def token_positions(pairs, first_row, count):
    index = first_row + jnp.arange(count, dtype=jnp.int32)
    owner = index // (2 * BLK)
    upper = index // BLK % 2
    offset = index % BLK
    ranks = pairs.shape[0]
    chosen = lax.optimization_barrier(jnp.sum(jnp.where(owner[:, None] == jnp.arange(ranks, dtype=jnp.int32)[None, :], pairs[None, :], 0), axis=1))
    block_number = jnp.where(upper == 0, chosen, 2 * ranks - 1 - chosen)
    return (block_number * BLK + offset).astype(jnp.int32)

def rope_tables(positions, head_width):
    half_width = head_width // 2
    ladder = jnp.arange(half_width, dtype=jnp.float32) * (2.0 / head_width)
    frequency = jnp.power(ROPE_BASE, -ladder)
    angle = positions.astype(jnp.float32)[:, None] * frequency[None, :]
    return (jnp.cos(angle), jnp.sin(angle))

def rotate(values, cosine, sine_part):
    half_width = values.shape[-1] // 2
    first_half = values[..., :half_width]
    second_half = values[..., half_width:]
    cosine = cosine[:, None, :]
    sine_part = sine_part[:, None, :]
    return jnp.concatenate([first_half * cosine - second_half * sine_part, second_half * cosine + first_half * sine_part], axis=-1)

def rms_scale(state, gain):
    inverse = lax.rsqrt(lax.optimization_barrier(jnp.mean(state * state, axis=-1, keepdims=True)) + EPSILON)
    return state * inverse * gain

def layer(state, gains, w_query, w_keyval, w_out, w_in, w_down, positions):
    length = state.shape[0]
    scale = HD ** (-0.5)
    first_normed = low(rms_scale(state, gains[0]))
    query_pre = low_back(jnp.dot(first_normed, w_query, precision=HIGHEST))
    keyval_pre = low_back(jnp.einsum('rd,dhc->rhc', first_normed, w_keyval, precision=HIGHEST))
    cosine, sine_part = rope_tables(positions, HD)
    query = low(rotate(query_pre.reshape(length, HQ, HD), cosine, sine_part))
    keys = low(rotate(keyval_pre[..., :HD], cosine, sine_part))
    values = low(keyval_pre[..., HD:])
    group = HQ // KVH
    allowed = positions[None, :] <= positions[:, None]
    head_keys = jnp.repeat(keys.transpose(1, 0, 2), group, axis=0)
    head_values = jnp.repeat(values.transpose(1, 0, 2), group, axis=0)

    def one_head(operands):
        head_query, key_rows, value_rows = operands
        scores = low_back(jnp.dot(head_query, key_rows.T, precision=HIGHEST) * scale)
        attention_weights = jax.nn.softmax(jnp.where(allowed, scores, MASKED), axis=-1)
        return jnp.dot(low(attention_weights), value_rows, precision=HIGHEST)
    heads = lax.map(jax.checkpoint(one_head), (query.transpose(1, 0, 2), head_keys, head_values))
    mixed = low(low_back(heads.transpose(1, 0, 2).reshape(length, HQ * HD)))
    state_mid = state + low_back(jnp.dot(mixed, w_out, precision=HIGHEST))
    second_normed = low(rms_scale(state_mid, gains[1]))
    gate_up = low_back(jnp.einsum('rd,dcf->rcf', second_normed, w_in, precision=HIGHEST))
    hidden = low(jax.nn.silu(gate_up[:, 0]) * gate_up[:, 1])
    return state_mid + low_back(jnp.dot(hidden, w_down, precision=HIGHEST))

def reference(boundary, pair_of_rank, norm_gains, w_query, w_keyval, w_out, w_in, w_down):
    positions = token_positions(pair_of_rank, 0, SEQ)
    params = tuple((weight.astype(jnp.float32) for weight in (norm_gains, w_query, w_keyval, w_out, w_in, w_down)))
    inputs = boundary[0].astype(jnp.float32)
    cotangent = boundary[1].astype(jnp.float32)

    def network(states, weights):
        first = tuple((weight[0] for weight in weights))
        second = tuple((weight[1] for weight in weights))
        results = []
        for micro in range(MICRO):
            middle = layer(states[micro], *first, positions)
            middle = low(low_back(middle))
            results.append(layer(middle, *second, positions))
        return jnp.stack(results)
    result, pullback = jax.vjp(network, inputs, params)
    grad_inputs, grad_params = pullback(cotangent)
    ends = jnp.stack([grad_inputs, result])
    return (ends, grad_params[0], grad_params[1], grad_params[2], grad_params[3], grad_params[4], grad_params[5])
```

```python
import jax
import jax.numpy as jnp
from jax import lax
from jax.experimental import pallas as pl
from jax.experimental.pallas import tpu as pltpu
from jax.sharding import PartitionSpec as P

HD = 64
BLK = 64
MICRO = 2
EPSILON = 1e-05
ROPE_BASE = 10000.0
MASKED = -1e30
WIDE = jnp.float32
NARROW = jnp.bfloat16
AXES = ("section", "ctx", "tp")


def rope_angles(positions):
    half_width = HD // 2
    ladder = jnp.arange(half_width, dtype=WIDE) * (2.0 / HD)
    frequency = jnp.power(ROPE_BASE, -ladder)
    return positions.astype(WIDE)[:, None] * frequency[None, :]


def keys_kernel(count):
    def kernel(*refs):
        cosine, sine_part, out = refs[count:]
        value = refs[0][...].astype(WIDE)
        for ref in refs[1:count]:
            value = value + ref[...].astype(WIDE)
        half_width = HD // 2
        lane = lax.broadcasted_iota(jnp.int32, value.shape, 1)
        after = pltpu.roll(value, 2 * HD - half_width, 1)
        before = pltpu.roll(value, half_width, 1)
        turned = jnp.where(lane < half_width, -after, before)
        out[...] = (value * cosine[...] + turned * sine_part[...]).astype(NARROW)

    return kernel


def turn_keys(pieces, cosine, sine_part):
    return pl.pallas_call(
        keys_kernel(len(pieces)),
        out_shape=jax.ShapeDtypeStruct(pieces[0].shape, NARROW),
        name="turn_keys",
    )(*pieces, cosine, sine_part)


def forward_kernel(count, length, heads):
    def kernel(*refs):
        query, key_refs = refs[0], refs[1 : 1 + count]
        cosine, sine_part, query_place, key_place = refs[1 + count : 5 + count]
        out, turned_query, log_total, store = refs[5 + count :]
        half_width = HD // 2
        allowed = key_place[...] <= query_place[...]
        allowed = jnp.concatenate([allowed.astype(WIDE)] * 2, axis=1) > 0.5
        cosine_here = cosine[...]
        sine_here = sine_part[...]
        for m in range(MICRO):
            span = pl.ds(m * length, length)
            columns = query[span, :].T * HD**-0.5
            for h in range(heads):
                first = columns[h * HD : h * HD + half_width]
                second = columns[h * HD + half_width : (h + 1) * HD]
                turned = jnp.concatenate(
                    [
                        first * cosine_here - second * sine_here,
                        second * cosine_here + first * sine_here,
                    ],
                    axis=0,
                )
                turned_query[h * HD : (h + 1) * HD, span] = turned.astype(NARROW)
            keyval = jnp.concatenate([ref[span, :] for ref in key_refs], axis=0)
            keyval_turned = keyval.T

            def pair(index, carry):
                base = pl.multiple_of(index * 2 * HD, 2 * HD)
                left = turned_query[pl.ds(base, HD), span]
                right = turned_query[pl.ds(base + HD, HD), span]
                both = jnp.concatenate([left, right], axis=1)
                both = jnp.concatenate([both, jnp.zeros_like(both)], axis=0)
                scores = dot(keyval, both)
                scores = jnp.where(allowed, scores, MASKED)
                top = jnp.max(scores, axis=0, keepdims=True)
                raised = jnp.exp(scores - top)
                total = jnp.sum(raised, axis=0, keepdims=True)
                mixed = dot(keyval_turned, raised.astype(NARROW))[HD:] / total
                store[pl.ds(base, HD), :] = mixed[:, :length]
                store[pl.ds(base + HD, HD), :] = mixed[:, length:]
                sums = top + jnp.log(total)
                log_total[index * 2, :, span] = sums[:, :length]
                log_total[index * 2 + 1, :, span] = sums[:, length:]
                return carry

            lax.fori_loop(0, heads // 2, pair, 0)
            out[span, :] = store[...].T.astype(NARROW)

    return kernel


def attention_forward(query, pieces, tables, heads, length):
    cosine, sine_part, query_place, key_place = tables
    rows = query.shape[0]
    return pl.pallas_call(
        forward_kernel(len(pieces), length, heads),
        out_shape=(
            jax.ShapeDtypeStruct((rows, heads * HD), NARROW),
            jax.ShapeDtypeStruct((heads * HD, rows), NARROW),
            jax.ShapeDtypeStruct((heads, 1, rows), WIDE),
        ),
        scratch_shapes=[pltpu.VMEM((heads * HD, length), WIDE)],
        name="attention_forward",
    )(query, *pieces, cosine, sine_part, query_place, key_place)


def backward_kernel(count, length, heads):
    def kernel(*refs):
        turned_query, grad_heads, log_total = refs[:3]
        key_refs = refs[3 : 3 + count]
        cosine, sine_part, query_place, key_place = refs[3 + count : 7 + count]
        grad_query = refs[7 + count]
        grad_key_refs = refs[8 + count : 8 + 2 * count]
        turned_grad, store, total = refs[8 + 2 * count :]
        half_width = HD // 2
        allowed = key_place[...] <= query_place[...]
        cosine_here = cosine[...]
        sine_here = sine_part[...]
        blank = jnp.zeros((HD, length), NARROW)
        for m in range(MICRO):
            span = pl.ds(m * length, length)
            turned_grad[...] = grad_heads[span, :].astype(WIDE).T.astype(NARROW)
            keyval = jnp.concatenate([ref[span, :] for ref in key_refs], axis=0)
            keyval_turned = keyval.T
            total[...] = jnp.zeros_like(total)

            def one(h, carry):
                base = pl.multiple_of(h * HD, HD)
                head_query = turned_query[pl.ds(base, HD), span]
                head_grad = turned_grad[pl.ds(base, HD), :]
                both = jnp.concatenate(
                    [
                        jnp.concatenate([head_query, blank], axis=1),
                        jnp.concatenate([blank, head_grad], axis=1),
                    ],
                    axis=0,
                )
                made = dot(keyval, both)
                scores = made[:, :length]
                grad_probs = made[:, length:]
                probs = jnp.where(allowed, jnp.exp(scores - log_total[h, :, span]), 0.0)
                delta = jnp.sum(probs * grad_probs, axis=0, keepdims=True)
                grad_scores = (probs * (grad_probs - delta)).astype(NARROW)
                pair = jnp.concatenate([grad_scores, probs.astype(NARROW)], axis=1)
                total[...] += dot(pair, both, 1, 1)
                columns = dot(keyval_turned, grad_scores)[:HD] * HD**-0.5
                first = columns[:half_width]
                second = columns[half_width:]
                store[pl.ds(base, HD), :] = jnp.concatenate(
                    [
                        first * cosine_here + second * sine_here,
                        second * cosine_here - first * sine_here,
                    ],
                    axis=0,
                )
                return carry

            lax.fori_loop(0, heads, one, 0)
            grad_query[span, :] = store[...].T.astype(NARROW)
            for k in range(count):
                grad_key_refs[k][span, :] = total[k * length : (k + 1) * length, :].astype(NARROW)

    return kernel


def attention_backward(turned_query, grad_heads, log_total, pieces, tables, heads, length):
    cosine, sine_part, query_place, key_place = tables
    rows = grad_heads.shape[0]
    count = len(pieces)
    results = pl.pallas_call(
        backward_kernel(count, length, heads),
        out_shape=(
            jax.ShapeDtypeStruct((rows, heads * HD), NARROW),
            *[jax.ShapeDtypeStruct((rows, 2 * HD), NARROW) for _ in range(count)],
        ),
        scratch_shapes=[
            pltpu.VMEM((heads * HD, length), NARROW),
            pltpu.VMEM((heads * HD, length), WIDE),
            pltpu.VMEM((count * length, 2 * HD), WIDE),
        ],
        name="attention_backward",
    )(
        turned_query,
        grad_heads,
        log_total,
        *pieces,
        cosine,
        sine_part,
        query_place,
        key_place,
    )
    return (results[0], list(results[1:]))


def fetch(chosen, sets, store, semaphores):
    count = len(sets[0])
    rows = sets[0][0].shape[0]

    def copies(index):
        return [
            pltpu.make_async_copy(
                sets[index][k], store.at[pl.ds(k * rows, rows), :], semaphores.at[k]
            )
            for k in range(count)
        ]

    for index in range(2):

        @pl.when(chosen[0] == index)
        def _():
            for copy in copies(index):
                copy.start()

    for copy in copies(0):
        copy.wait()


def ffn_grads_kernel(count, tiles, layout):
    cut, heads_width, hidden_width = layout

    def kernel(*refs):
        chosen, packs = refs[0], refs[1 : 1 + count]
        sets = (refs[1 + count : 1 + 2 * count], refs[1 + 2 * count : 1 + 3 * count])
        grad_in, grad_down, store, semaphores = refs[1 + 3 * count :]
        step = pl.program_id(0)

        @pl.when(step == 0)
        def _():
            fetch(chosen, sets, store, semaphores)

        base = cut + heads_width
        width = hidden_width // tiles
        inputs = jnp.concatenate([pack[:, base : base + cut] for pack in packs], axis=0)
        start = pl.multiple_of(cut + step * 2 * width, 128)
        grad_in[...] = dot(inputs, store[:, pl.ds(start, 2 * width)], 0, 0)
        start = pl.multiple_of(base + cut + step * width, 128)
        hidden = jnp.concatenate([pack[:, pl.ds(start, width)] for pack in packs], axis=0)
        grad_down[...] = dot(hidden, store[:, :cut], 0, 0)

    return kernel


def whole_block(shape):
    return pl.BlockSpec(shape, lambda *_: (0, 0), pipeline_mode=pl.Buffered(1))


def ffn_grads(chosen, packs, early, late, layout):
    cut, heads_width, hidden_width = layout
    count = len(packs)
    tiles = hidden_width // 128
    rows = packs[0].shape[0]
    return pl.pallas_call(
        ffn_grads_kernel(count, tiles, layout),
        grid=(tiles,),
        in_specs=[pl.BlockSpec(memory_space=pltpu.SMEM)]
        + [whole_block(pack.shape) for pack in packs]
        + [pl.BlockSpec(memory_space=pl.ANY)] * (2 * count),
        out_specs=[
            pl.BlockSpec((cut, 256), lambda i: (0, i)),
            pl.BlockSpec((128, cut), lambda i: (i, 0)),
        ],
        out_shape=(
            jax.ShapeDtypeStruct((cut, 2 * hidden_width), WIDE),
            jax.ShapeDtypeStruct((hidden_width, cut), WIDE),
        ),
        scratch_shapes=[
            pltpu.VMEM((count * rows, early[0].shape[1]), NARROW),
            pltpu.SemaphoreType.DMA((count,)),
        ],
        name="ffn_grads",
    )(chosen, *packs, *early, *late)


def attention_grads_kernel(count, layout):
    cut, heads_width, _ = layout

    def kernel(*refs):
        chosen, packs = refs[0], refs[1 : 1 + count]
        sets = (refs[1 + count : 1 + 2 * count], refs[1 + 2 * count : 1 + 3 * count])
        grad_out, grad_query, grad_keyval, store, semaphores = refs[1 + 3 * count :]
        fetch(chosen, sets, store, semaphores)
        heads = jnp.concatenate([pack[:, cut : cut + heads_width] for pack in packs], axis=0)
        grad_out[...] = dot(heads, store[:, :cut], 0, 0)
        inputs = jnp.concatenate([pack[:, :cut] for pack in packs], axis=0)
        made = dot(inputs, store[:, cut:], 0, 0)
        grad_query[...] = made[:, :heads_width]
        grad_keyval[...] = made[:, heads_width:]

    return kernel


def attention_grads(chosen, packs, early, late, layout):
    cut, heads_width, _ = layout
    count = len(packs)
    rows = packs[0].shape[0]
    return pl.pallas_call(
        attention_grads_kernel(count, layout),
        grid=(1,),
        in_specs=[pl.BlockSpec(memory_space=pltpu.SMEM)]
        + [whole_block((rows, cut + heads_width)) for _ in packs]
        + [pl.BlockSpec(memory_space=pl.ANY)] * (2 * count),
        out_specs=[
            whole_block((heads_width, cut)),
            whole_block((cut, heads_width)),
            whole_block((cut, 2 * HD)),
        ],
        out_shape=(
            jax.ShapeDtypeStruct((heads_width, cut), WIDE),
            jax.ShapeDtypeStruct((cut, heads_width), WIDE),
            jax.ShapeDtypeStruct((cut, 2 * HD), WIDE),
        ),
        scratch_shapes=[
            pltpu.VMEM((count * rows, early[0].shape[1]), NARROW),
            pltpu.SemaphoreType.DMA((count,)),
        ],
        name="attention_grads",
    )(chosen, *packs, *early, *late)


def norm_forward(state, gain):
    inverse = lax.rsqrt(jnp.mean(state * state, axis=1, keepdims=True) + EPSILON)
    return (inverse, (state * inverse * gain).astype(NARROW))


def norm_backward(grad_normed, state, inverse, gain):
    scaled = grad_normed * gain
    gain_grad = jnp.sum(grad_normed * state * inverse, axis=0)
    grad_state = inverse * scaled - state * inverse**3 * jnp.mean(
        scaled * state, axis=1, keepdims=True
    )
    return (gain_grad, grad_state)


def dot(left, right, left_dim=1, right_dim=0):
    return lax.dot_general(
        left, right, (((left_dim,), (right_dim,)), ((), ())), preferred_element_type=WIDE
    )


def solution(mesh):
    sizes = {axis: mesh.shape[axis] for axis in AXES}

    def moves(axis, step, active):
        sections = range(sizes["section"]) if active is None else (active,)

        def number(s, c, t):
            return (s * sizes["ctx"] + c) * sizes["tp"] + t

        result = []
        for s in sections:
            for c in range(sizes["ctx"]):
                for t in range(sizes["tp"]):
                    if axis == "ctx":
                        target = number(s, c ^ step, t)
                    else:
                        target = number(s, c, t ^ step)
                    result.append((number(s, c, t), target))
        return result

    def swapped(value, axis, step, active):
        return lax.ppermute(value, AXES, moves(axis, step, active))

    def gathered(value, axis, active):
        return [value] + [swapped(value, axis, k, active) for k in range(1, sizes[axis])]

    def scattered(pieces, axis, active):
        moved = [swapped(pieces[k], axis, k, active) for k in range(1, sizes[axis])]
        total = pieces[0].astype(WIDE)
        for piece in moved:
            total = total + piece.astype(WIDE)
        return total

    def crossing(value, source):
        half = sizes["ctx"] * sizes["tp"]
        first = source * half
        second = (1 - source) * half
        return lax.ppermute(value, AXES, [(first + i, second + i) for i in range(half)])

    def body(boundary, pair_of_rank, norm_gains, w_query, w_keyval, w_out, w_in, w_down):
        n_ctx, n_tp = sizes["ctx"], sizes["tp"]
        rows = boundary.shape[2]
        width = boundary.shape[3]
        own_rows = MICRO * rows
        heads_here = w_query.shape[2] // HD
        hidden_here = w_down.shape[1]
        slice_width = width // n_ctx
        gains = norm_gains[0].astype(WIDE)
        weight_query = w_query[0]
        weight_keyval = w_keyval[0].reshape(width, -1)
        weight_out = w_out[0]
        weight_in = w_in[0].reshape(width, -1)
        weight_down = w_down[0]
        section = lax.axis_index("section")
        rank = lax.axis_index("ctx")
        part = lax.axis_index("tp")
        first_section = section == 0

        def positions_of(rank_index):
            chosen = jnp.sum(
                jnp.where(jnp.arange(n_ctx, dtype=jnp.int32) == rank_index, pair_of_rank, 0)
            )
            places = []
            for j in range(n_tp):
                index = (part ^ j) * rows + jnp.arange(rows, dtype=jnp.int32)
                block = jnp.where(index // BLK % 2 == 0, chosen, 2 * n_ctx - 1 - chosen)
                places.append(block * BLK + index % BLK)
            return jnp.stack(places)

        length = n_tp * rows
        own_places = positions_of(rank).reshape(-1)
        key_places = jnp.concatenate([positions_of(rank ^ k).reshape(-1) for k in range(n_ctx)])
        angles = rope_angles(own_places)
        tables = (
            jnp.cos(angles).T,
            jnp.sin(angles).T,
            own_places[None, :],
            key_places[:, None],
        )
        row_angles = jnp.concatenate([jnp.concatenate([angles, angles], axis=1)] * MICRO)
        key_cosine = jnp.concatenate([jnp.cos(row_angles), jnp.ones_like(row_angles)], axis=1)
        key_sine = jnp.concatenate([jnp.sin(row_angles), jnp.zeros_like(row_angles)], axis=1)

        def parts_of(value):
            return [
                jnp.concatenate(
                    [
                        value[m * length + j * rows : m * length + (j + 1) * rows]
                        for m in range(MICRO)
                    ]
                )
                for j in range(n_tp)
            ]

        def whole_of(pieces):
            return jnp.concatenate(
                [piece[m * rows : (m + 1) * rows] for m in range(MICRO) for piece in pieces]
            )

        def forward(state, active):
            first_inverse, first_normed = norm_forward(state, gains[0])
            attention_in = whole_of(gathered(first_normed, "tp", active))
            keyval = turn_keys([dot(attention_in, weight_keyval)], key_cosine, key_sine)
            pieces = gathered(keyval, "ctx", active)
            query_pre = dot(attention_in, weight_query)
            heads_low, query, log_total = attention_forward(
                query_pre, pieces, tables, heads_here, length
            )
            mixed = dot(heads_low, weight_out).astype(NARROW)
            state_mid = state + scattered(parts_of(mixed), "tp", active)
            second_inverse, second_normed = norm_forward(state_mid, gains[1])
            ffn_in = whole_of(gathered(second_normed, "tp", active))
            gate_up = dot(ffn_in, weight_in)
            gate = gate_up[:, :hidden_here]
            hidden = (jax.nn.silu(gate) * gate_up[:, hidden_here:]).astype(NARROW)
            lowered = dot(hidden, weight_down).astype(NARROW)
            state_out = state_mid + scattered(parts_of(lowered), "tp", active)
            kept = dict(
                state=state,
                first_inverse=first_inverse,
                attention_in=attention_in,
                query=query,
                pieces=pieces,
                log_total=log_total,
                heads_low=heads_low,
                state_mid=state_mid,
                second_inverse=second_inverse,
                ffn_in=ffn_in,
                gate_up=gate_up,
                hidden=hidden,
            )
            return (state_out, kept)

        def backward(grad, kept, active):
            grad_ffn = whole_of(gathered(grad.astype(NARROW), "tp", active))
            grad_hidden = dot(grad_ffn, weight_down, 1, 1)
            gate = kept["gate_up"][:, :hidden_here]
            up_part = kept["gate_up"][:, hidden_here:]
            sigma = jax.nn.sigmoid(gate)
            grad_gate = grad_hidden * up_part * sigma * (1.0 + gate * (1.0 - sigma))
            grad_up = grad_hidden * gate * sigma
            grad_gate_up = jnp.concatenate([grad_gate, grad_up], axis=1).astype(NARROW)
            partial = dot(grad_gate_up, weight_in, 1, 1).astype(NARROW)
            grad_second = scattered(parts_of(partial), "tp", active)
            second_gain, grad_mid = norm_backward(
                grad_second, kept["state_mid"], kept["second_inverse"], gains[1]
            )
            grad_mid = grad_mid + grad
            grad_attention = whole_of(gathered(grad_mid.astype(NARROW), "tp", active))
            grad_heads = dot(grad_attention, weight_out, 1, 1).astype(NARROW)
            grad_query_pre, grad_pieces = attention_backward(
                kept["query"],
                grad_heads,
                kept["log_total"],
                kept["pieces"],
                tables,
                heads_here,
                length,
            )
            moved = [grad_pieces[0]] + [
                swapped(grad_pieces[k], "ctx", k, active) for k in range(1, n_ctx)
            ]
            grad_keyval_pre = turn_keys(moved, key_cosine, -key_sine)
            partial = (
                dot(grad_query_pre, weight_query, 1, 1)
                + dot(grad_keyval_pre, weight_keyval, 1, 1)
            ).astype(NARROW)
            grad_first = scattered(parts_of(partial), "tp", active)
            first_gain, grad_in = norm_backward(
                grad_first, kept["state"], kept["first_inverse"], gains[0]
            )
            grad_in = grad_in + grad_mid
            return (
                grad_in,
                jnp.stack([first_gain, second_gain]),
                dict(
                    grad_ffn=grad_ffn,
                    grad_gate_up=grad_gate_up,
                    grad_attention=grad_attention,
                    grad_query_pre=grad_query_pre,
                    grad_keyval_pre=grad_keyval_pre,
                ),
            )

        def column_slice(value, index):
            return lax.dynamic_slice_in_dim(value, index * slice_width, slice_width, 1)

        def packed(columns, whole, active):
            made = []
            for k in range(n_ctx):
                pack = jnp.concatenate([column_slice(columns, rank ^ k), *whole], axis=1)
                made.append(swapped(pack, "ctx", k, active) if k else pack)
            return made

        boundary_rows = boundary[0].reshape(own_rows, width).astype(WIDE)
        middle, kept_first = forward(boundary_rows, 0)
        received = crossing(middle.astype(NARROW), 0).astype(WIDE)
        output, kept_second = forward(received, 1)

        own = {
            name: jnp.where(first_section, kept_first[name], kept_second[name])
            for name in ("attention_in", "heads_low", "ffn_in", "hidden")
        }
        packs = []
        for k in range(n_ctx):
            pack = jnp.concatenate(
                [
                    column_slice(own["attention_in"], rank ^ k),
                    own["heads_low"],
                    column_slice(own["ffn_in"], rank ^ k),
                    own["hidden"],
                ],
                axis=1,
            )
            packs.append(swapped(pack, "ctx", k, None) if k else pack)

        def backward_packs(moved, active):
            return (
                packed(moved["grad_ffn"], [moved["grad_gate_up"]], active),
                packed(
                    moved["grad_attention"],
                    [moved["grad_query_pre"], moved["grad_keyval_pre"]],
                    active,
                ),
            )

        grad_middle, gains_second, moved_second = backward(boundary_rows, kept_second, 1)
        late = backward_packs(moved_second, 1)
        received = crossing(grad_middle.astype(NARROW), 1).astype(WIDE)
        grad_input, gains_first, moved_first = backward(received, kept_first, 0)
        early = backward_packs(moved_first, 0)
        chosen = section.astype(jnp.int32).reshape(1)
        layout = (slice_width, heads_here * HD, hidden_here)
        total_in, total_down = ffn_grads(chosen, packs, early[0], late[0], layout)
        total_out, total_query, total_keyval = attention_grads(
            chosen, packs, early[1], late[1], layout
        )
        gain_parts = jnp.where(first_section, gains_first, gains_second)
        gain_total = scattered([column_slice(gain_parts, rank ^ k) for k in range(n_ctx)], "ctx", None)
        gain_total = scattered([gain_total] * n_tp, "tp", None)
        ends = jnp.where(first_section, grad_input, output).reshape(1, MICRO, rows, width)
        return (
            ends,
            gain_total[None],
            total_query[None],
            total_keyval.reshape(1, slice_width, w_keyval.shape[2], w_keyval.shape[3]),
            total_out[None],
            total_in.reshape(1, slice_width, 2, hidden_here),
            total_down[None],
        )

    placed = (
        P("section", None, ("ctx", "tp"), None),
        P(),
        P("section", None, None),
        P("section", None, "tp"),
        P("section", None, "tp", None),
        P("section", "tp", None),
        P("section", None, None, "tp"),
        P("section", "tp", None),
    )
    return jax.shard_map(
        body,
        mesh=mesh,
        in_specs=placed,
        out_specs=(
            P("section", None, ("ctx", "tp"), None),
            P("section", None, "ctx"),
            P("section", "ctx", "tp"),
            P("section", "ctx", "tp", None),
            P("section", "tp", "ctx"),
            P("section", "ctx", None, "tp"),
            P("section", "tp", "ctx"),
        ),
        check_vma=False,
    )
```
